32 devices in a mesh: groups: 2 (over x), row: 16 (over z, y, core).
Axes of the slice: x: 2, y: 2, z: 4, core: 2. Of those that a mesh axis runs over, the one named last changes fastest.
Arguments:
- features: bfloat16 [16384, 128], P(('groups', 'row')), parts along dimension 0, may hold values from -6 to 6
- weight: bfloat16 [128, 256], replicated, may hold values from -0.5 to 0.5
- block_cols: int32 [128, 16], P(('groups', 'row')), parts along dimension 0, may hold values from 0 to 63, as said below
- block_counts: int32 [128], P(('groups', 'row')), parts along dimension 0, may hold values from 1 to 16, as said below
- block_vals: bfloat16 [128, 16, 128, 128], P(('groups', 'row')), parts along dimension 0, may hold values from 0 to 0.03125, as said below
- out_grad: bfloat16 [16384, 256], P(('groups', 'row')), parts along dimension 0, may hold values from -6 to 6
Outputs:
- hidden_out: bfloat16 [16384, 256], P(('groups', 'row')), parts along dimension 0
- feat_grad: bfloat16 [16384, 128], P(('groups', 'row')), parts along dimension 0
- weight_grad: float32 [256, 256], P('groups'), parts along dimension 0
The draws below stay inside these ranges and needn't reach their ends.
There are 2 independent parts, one for each index of `groups`. The reference program is written for one: setup_inputs(seed, part) draws one part's arguments, and reference() takes and returns one part's arrays. A program takes and returns all parts, laid end to end along the dimension named above; an argument that names none is the same for every part. Nothing has to cross between parts.
Inputs may be any that keep to these rules, and one draw needn't show every extreme that they name: `block_cols`: within a row panel the first block_counts entries are distinct block columns; entries past the count are valid indices but are not part of A. `block_counts`: some panel holds exactly 16 blocks. `block_vals`: A is symmetric: where panel p stores a block at block column q, panel q stores the transposed block at block column p.
All inputs are finite; a program needn't handle non-finite values.
Results may differ from the reference program's by a relative error of at most 0.005.
Values may be sent and summed in bfloat16 or wider, within the bound.
No kernel may reach another device: no remote copies, remote signals or barrier semaphores. Data moves between devices by JAX's collectives and lax.ppermute only.
A program may use at most 64 MiB of HBM per device.

```python
import jax
import jax.numpy as jnp
from jax import lax

FIN = 128
FOUT = 256
BLK = 128
MAXB = 16
ROWS_DEV = 512
NODES = 8192
PANELS = 64


def graph_layout(key):
    panel_total = PANELS
    half_way = panel_total // 2
    pairs = (MAXB - 2) // 2
    near = ROWS_DEV // BLK
    base = jax.random.fold_in(key, 41)
    others = jax.random.permutation(jax.random.fold_in(base, 1), half_way - 2) + 1
    others = jnp.where(others >= near, others + 1, others)
    offsets = jnp.concatenate([jnp.full((1,), near, dtype=jnp.int32), others[:pairs - 1].astype(jnp.int32)])
    first = jax.random.randint(jax.random.fold_in(base, 2), (panel_total,), 0, pairs + 1)
    second = jax.random.randint(jax.random.fold_in(base, 3), (panel_total,), 0, pairs + 1)
    levels = first * second // pairs
    chosen = jax.random.randint(jax.random.fold_in(base, 4), (), 0, panel_total)
    beside_all = jnp.concatenate([chosen[None], (chosen + offsets) % panel_total, (chosen - offsets) % panel_total, ((chosen + half_way) % panel_total)[None]])
    position = jnp.arange(panel_total, dtype=jnp.int32)
    forced = jnp.any(position[:, None] == beside_all[None, :], axis=1)
    levels = jnp.where(forced, pairs, levels)
    ahead = (position[:, None] + offsets[None, :]) % panel_total
    behind = (position[:, None] - offsets[None, :]) % panel_total
    far_col = (position + half_way) % panel_total
    stepper = jnp.arange(pairs, dtype=jnp.int32)[None, :]
    keep_ahead = stepper < jnp.minimum(levels[:, None], levels[ahead])
    keep_behind = stepper < jnp.minimum(levels[:, None], levels[behind])
    keep_far = jnp.minimum(levels, levels[far_col]) > 0
    columns = jnp.concatenate([position[:, None], jnp.stack([ahead, behind], axis=2).reshape(panel_total, 2 * pairs), far_col[:, None]], axis=1)
    present = jnp.concatenate([jnp.ones((panel_total, 1), dtype=bool), jnp.stack([keep_ahead, keep_behind], axis=2).reshape(panel_total, 2 * pairs), keep_far[:, None]], axis=1)
    score = jnp.where(present, 0, MAXB) + jnp.arange(MAXB, dtype=jnp.int32)[None, :]
    order = jnp.argsort(score, axis=1)
    return (columns, present, order, offsets)


def draw_block_cols(key, part):
    columns, present, order, offsets = graph_layout(key)
    return jnp.take_along_axis(columns, order, axis=1).astype(jnp.int32)


def draw_block_counts(key, part):
    columns, present, order, offsets = graph_layout(key)
    return jnp.sum(present.astype(jnp.int32), axis=1).astype(jnp.int32)


def draw_block_vals(key, part):
    columns, present, order, offsets = graph_layout(key)
    panel_total = PANELS
    half_way = panel_total // 2
    pairs = (MAXB - 2) // 2
    value_key = jax.random.fold_in(key, 59)
    forward = jax.random.uniform(jax.random.fold_in(value_key, 1), (panel_total, pairs, BLK, BLK), jnp.float32, 0.0, 4.0 / BLK)
    own = jax.random.uniform(jax.random.fold_in(value_key, 2), (panel_total, BLK, BLK), jnp.float32, 0.0, 4.0 / BLK)
    own = 0.5 * (own + jnp.swapaxes(own, 1, 2))
    far_draw = jax.random.uniform(jax.random.fold_in(value_key, 3), (panel_total, BLK, BLK), jnp.float32, 0.0, 4.0 / BLK)
    position = jnp.arange(panel_total, dtype=jnp.int32)
    partner = (position + half_way) % panel_total
    far_vals = jnp.where((position < half_way)[:, None, None], far_draw, jnp.swapaxes(far_draw[partner], 1, 2))
    source = (position[:, None] - offsets[None, :]) % panel_total
    backward = jnp.swapaxes(forward[source, jnp.arange(pairs, dtype=jnp.int32)[None, :]], -1, -2)
    slots = jnp.stack([forward, backward], axis=2).reshape(panel_total, 2 * pairs, BLK, BLK)
    full = jnp.concatenate([own[:, None], slots, far_vals[:, None]], axis=1)
    ordered = jnp.take_along_axis(full, order[:, :, None, None], axis=1)
    return ordered.astype(jnp.bfloat16)


def block_scale(key, dims, split, low, largest):
    factor_of, own = 1.0, jax.random.fold_in(key, 6)
    for dim, blocks in split:
        draws = jnp.exp(jax.random.uniform(jax.random.fold_in(own, dim), (blocks,), jnp.float32, low / len(split), largest / len(split)))
        factor_of = factor_of * jnp.repeat(draws, dims[dim] // blocks).reshape([-1 if axis == dim else 1 for axis in range(len(dims))])
    return factor_of


def gaussian(rng, shape, spread, reach, split=(), kind=jnp.bfloat16):
    result = jax.random.normal(rng, shape, jnp.float32) * spread
    if len(split) > 0:
        result = block_scale(rng, shape, split, -0.22, 0.18) * result
    return jnp.clip(result, min=-reach, max=reach).astype(kind)


def setup_inputs(seed: int = 0, part: int = 0) -> dict:
    seeds = jax.random.split(jax.random.key(seed), 7)
    own_keys = jax.random.split(jax.random.fold_in(seeds[6], part), 7)
    features = gaussian(own_keys[0], (NODES, FIN), 1.0, 6.0, ((0, 16),))
    weight = gaussian(seeds[1], (FIN, FOUT), FIN ** -0.5, 0.5)
    block_cols = draw_block_cols(jax.random.fold_in(jax.random.fold_in(seeds[6], part), 71), part)
    block_counts = draw_block_counts(jax.random.fold_in(jax.random.fold_in(seeds[6], part), 71), part)
    block_vals = draw_block_vals(jax.random.fold_in(jax.random.fold_in(seeds[6], part), 71), part)
    out_grad = gaussian(own_keys[5], (NODES, FOUT), 1.0, 6.0, ((0, 16),))
    return {"features": features, "weight": weight, "block_cols": block_cols, "block_counts": block_counts, "block_vals": block_vals, "out_grad": out_grad}


def reference(features, weight, block_cols, block_counts, block_vals, out_grad):
    panel_total, slot_count, block_side, _ = block_vals.shape
    in_width = features.shape[1]
    col_blocks = features.shape[0] // block_side
    in_use = jnp.arange(slot_count, dtype=jnp.int32)[None, :] < block_counts[:, None]
    blocks = jnp.where(in_use[:, :, None, None], block_vals.astype(jnp.float32), jnp.float32(0.0))
    picked = features.reshape(col_blocks, block_side, in_width)[block_cols].astype(jnp.float32)
    aggregated = jnp.einsum('pbij,pbjf->pif', blocks, picked, precision=lax.Precision.HIGHEST).reshape(-1, in_width)
    weight_wide = weight.astype(jnp.float32)
    preact = jnp.dot(aggregated, weight_wide, precision=lax.Precision.HIGHEST)
    hidden, pullback = jax.vjp(jax.nn.gelu, preact)
    pre_grad = pullback(out_grad.astype(jnp.float32))[0]
    weight_grad = jnp.dot(aggregated.T, pre_grad, precision=lax.Precision.HIGHEST)
    edge_grad = jnp.dot(pre_grad, weight_wide.T, precision=lax.Precision.HIGHEST).astype(jnp.bfloat16)
    edge_grad = lax.optimization_barrier(edge_grad).astype(jnp.float32)
    contrib = jnp.einsum('pbij,pif->pbjf', blocks, edge_grad.reshape(panel_total, block_side, in_width), precision=lax.Precision.HIGHEST)
    feat_term = jax.ops.segment_sum(contrib.reshape(panel_total * slot_count, block_side, in_width), block_cols.reshape(-1), num_segments=col_blocks)
    feat_grad = feat_term.reshape(-1, in_width).astype(jnp.bfloat16)
    return (hidden.astype(jnp.bfloat16), feat_grad, weight_grad)
```

```python
import jax
import jax.numpy as jnp
from jax import lax
from jax.experimental import pallas as pl
from jax.experimental.pallas import tpu as pltpu
from jax.sharding import PartitionSpec as P

GROUP = 4
GELU_C = 0.7978845608028654
GELU_A = 0.044715


def in_vmem(x):
    return pltpu.with_memory_space_constraint(x, pltpu.VMEM)


def exchange(x, bit, size):
    return lax.ppermute(x, "row", [(i, i ^ bit) for i in range(size)])


def gather_rows(x, size):
    if size != 16:
        return [(None, lax.all_gather(x, "row", axis=0, tiled=True))]
    held = {0: x}
    held[8] = exchange(x, 8, size)
    held[4] = exchange(x, 4, size)
    held[12] = exchange(held[8], 4, size)
    for mask in (0, 4, 8, 12):
        held[mask ^ 2] = exchange(held[mask], 2, size)
    for mask in (0, 2, 4, 6, 8, 10, 12, 14):
        held[mask ^ 1] = exchange(held[mask], 1, size)
    return sorted(held.items())


def row_sum(keep, send, core, size):
    total = keep + exchange(send, 1, size)
    bit = size // 2
    while bit > 1:
        total = total + exchange(total, bit, size)
        bit //= 2
    other = exchange(total, 1, size)
    return jnp.where(
        core == 0, jnp.concatenate([total, other], 0), jnp.concatenate([other, total], 0)
    )


def collect(me, masks, pieces, nodes):
    if nodes is None:
        return pieces[0]
    rows = pieces[0].shape[0]
    for mask, piece in zip(masks, pieces):
        blocks = piece.shape[0]
        start = (me ^ mask) * blocks
        for i in range(blocks):
            nodes[start + i] = piece[i]
    return nodes


def panel_product(cols, counts, vals, nodes, panel):
    used = counts[panel]
    side = vals.shape[2]

    def product(b):
        return jnp.dot(
            vals[panel, b], nodes[cols[panel, b]], preferred_element_type=jnp.float32
        )

    def many(step, total):
        for j in range(GROUP):
            total = total + product(step * GROUP + j)
        return total

    full = used // GROUP
    total = lax.fori_loop(0, full, many, jnp.zeros((side, nodes.shape[2]), jnp.float32))
    return lax.fori_loop(full * GROUP, used, lambda b, t: t + product(b), total)


def split(x):
    high = x.astype(jnp.bfloat16)
    return high, (x - high.astype(jnp.float32)).astype(jnp.bfloat16)


def dot(a, b, dims):
    return lax.dot_general(a, b, (dims, ((), ())), preferred_element_type=jnp.float32)


def forward_kernel(masks, *refs):
    n = len(masks)
    me, cols, counts = refs[:3]
    pieces = refs[3 : 3 + n]
    vals, weight, out_grad = refs[3 + n : 6 + n]
    hidden, edge, keep, send = refs[6 + n : 10 + n]
    wsum = refs[10 + n]
    nodes = collect(me[0], masks, pieces, refs[11 + n] if n > 1 else None)
    panels, _, side, _ = vals.shape
    half = keep.shape[0]
    w = weight[...]
    for panel in range(panels):
        rows = pl.ds(panel * side, side)
        agg = panel_product(cols, counts, vals, nodes, panel)
        agg_h, agg_l = split(agg)
        z = dot(agg_h, w, ((1,), (0,))) + dot(agg_l, w, ((1,), (0,)))
        zz = z * z
        t = jnp.tanh(z * (GELU_C + (GELU_C * GELU_A) * zz))
        half_up = 0.5 + 0.5 * t
        hidden[rows, :] = (z * half_up).astype(jnp.bfloat16)
        slope = half_up + (0.5 * z) * (1.0 - t * t) * (GELU_C + (3.0 * GELU_C * GELU_A) * zz)
        dz = out_grad[rows, :].astype(jnp.float32) * slope
        dz_h, dz_l = split(dz)
        edge[panel] = (dot(dz_h, w, ((1,), (1,))) + dot(dz_l, w, ((1,), (1,)))).astype(jnp.bfloat16)
        part = (
            dot(agg_h, dz_h, ((0,), (0,)))
            + dot(agg_l, dz_h, ((0,), (0,)))
            + dot(agg_h, dz_l, ((0,), (0,)))
        )
        wsum[...] = part if panel == 0 else wsum[...] + part
    core = me[0] % 2
    keep[...] = wsum[pl.ds(pl.multiple_of(core * half, half), half), :]
    send[...] = wsum[pl.ds(pl.multiple_of((1 - core) * half, half), half), :]


def backward_kernel(masks, *refs):
    n = len(masks)
    me, cols, counts = refs[:3]
    pieces = refs[3 : 3 + n]
    vals = refs[3 + n]
    feat = refs[4 + n]
    nodes = collect(me[0], masks, pieces, refs[5 + n] if n > 1 else None)
    panels, _, side, _ = vals.shape
    for panel in range(panels):
        rows = pl.ds(panel * side, side)
        feat[rows, :] = panel_product(cols, counts, vals, nodes, panel).astype(jnp.bfloat16)


PARAMS = pltpu.CompilerParams(vmem_limit_bytes=12 * 2**20)
SMEM = pl.BlockSpec(memory_space=pltpu.SMEM)
VMEM = pl.BlockSpec(memory_space=pltpu.VMEM)


def body(features, weight, block_cols, block_counts, block_vals, out_grad):
    size = lax.axis_size("row")
    panels, _, side, _ = block_vals.shape
    rows, width = features.shape
    hidden_width = weight.shape[1]
    node_blocks = size * panels
    me = lax.axis_index("row").astype(jnp.int32).reshape(1)
    vals = in_vmem(block_vals)

    def gathered(x):
        held = gather_rows(x.reshape(panels, side, width), size)
        scratch = []
        if len(held) > 1:
            scratch = [pltpu.VMEM((node_blocks, side, width), jnp.bfloat16)]
        return tuple(m for m, _ in held), [in_vmem(a) for _, a in held], scratch

    masks, pieces, scratch = gathered(features)
    hidden, edge, keep, send = pl.pallas_call(
        lambda *refs: forward_kernel(masks, *refs),
        name="forward",
        compiler_params=PARAMS,
        out_shape=(
            jax.ShapeDtypeStruct((rows, hidden_width), jnp.bfloat16),
            jax.ShapeDtypeStruct((panels, side, width), jnp.bfloat16),
            jax.ShapeDtypeStruct((width // 2, hidden_width), jnp.float32),
            jax.ShapeDtypeStruct((width // 2, hidden_width), jnp.float32),
        ),
        in_specs=[SMEM] * 3 + [VMEM] * (len(pieces) + 3),
        out_specs=(VMEM,) * 4,
        scratch_shapes=[pltpu.VMEM((width, hidden_width), jnp.float32)] + scratch,
    )(me, block_cols, block_counts, *pieces, vals, in_vmem(weight), in_vmem(out_grad))

    masks, pieces, scratch = gathered(edge)
    feat_grad = pl.pallas_call(
        lambda *refs: backward_kernel(masks, *refs),
        name="backward",
        compiler_params=PARAMS,
        out_shape=jax.ShapeDtypeStruct((rows, width), jnp.bfloat16),
        in_specs=[SMEM] * 3 + [VMEM] * (len(pieces) + 1),
        out_specs=VMEM,
        scratch_shapes=scratch,
    )(me, block_cols, block_counts, *pieces, vals)
    weight_grad = row_sum(keep, send, me[0] % 2, size)
    return hidden, feat_grad, weight_grad


def solution(mesh):
    in_specs = (
        P(("groups", "row"), None),
        P(),
        P(("groups", "row"), None),
        P(("groups", "row")),
        P(("groups", "row"), None, None, None),
        P(("groups", "row"), None),
    )
    out_specs = (P(("groups", "row"), None), P(("groups", "row"), None), P("groups", None))
    return jax.shard_map(body, mesh=mesh, in_specs=in_specs, out_specs=out_specs, check_vma=False)
```

```python
import jax
import jax.numpy as jnp
from jax import lax
from jax.experimental import pallas as pl
from jax.experimental.pallas import tpu as pltpu
from jax.sharding import PartitionSpec as P

GROUP = 4
GELU_C = 0.7978845608028654
GELU_A = 0.044715
PARAMS = pltpu.CompilerParams(vmem_limit_bytes=12 * 2**20)
SMEM = pl.BlockSpec(memory_space=pltpu.SMEM)
VMEM = pl.BlockSpec(memory_space=pltpu.VMEM)


def in_vmem(x):
    return pltpu.with_memory_space_constraint(x, pltpu.VMEM)


def stage(*arrays):
    n = len(arrays)

    def kernel(*refs):
        sems = refs[2 * n]
        copies = [
            pltpu.make_async_copy(refs[i], refs[n + i], sems.at[i]) for i in range(n)
        ]
        for c in copies:
            c.start()
        for c in copies:
            c.wait()

    return pl.pallas_call(
        kernel,
        name="stage",
        compiler_params=PARAMS,
        out_shape=tuple(pltpu.VMEM(a.shape, a.dtype) for a in arrays),
        in_specs=[pl.BlockSpec(memory_space=pltpu.HBM)] * n,
        out_specs=(VMEM,) * n,
        scratch_shapes=[pltpu.SemaphoreType.DMA((n,))],
    )(*(pltpu.with_memory_space_constraint(a, pltpu.HBM) for a in arrays))


def exchange(x, bit, size):
    return lax.ppermute(x, "row", [(i, i ^ bit) for i in range(size)])


def after(x, *others):
    return lax.optimization_barrier((x, *others))[0]


def gather_rows(x, own, size, staged=None):
    if size != 16:
        return [(None, lax.all_gather(x, "row", axis=0, tiled=True))]
    held = {0: x}
    held[8] = exchange(x, 8, size)
    held[4] = exchange(x, 4, size)
    far = held[8] if staged is None else after(held[8], staged)
    held[12] = exchange(far, 4, size)
    for mask in (0, 4, 8, 12):
        held[mask ^ 2] = exchange(held[mask], 2, size)
    for mask in (0, 2, 4, 6, 8, 10, 12, 14):
        held[mask ^ 1] = exchange(held[mask], 1, size)
    held[0] = own
    return sorted(held.items())


def row_sum(keep, send, held, size):
    held = dict(held)
    total = keep + exchange(send, 1, size)
    if size == 16:
        total = total + exchange(after(total, held[4]), 2, size)
        total = total + exchange(total, 4, size)
        total = total + exchange(after(total, held[8]), 8, size)
    else:
        bit = size // 2
        while bit > 1:
            total = total + exchange(total, bit, size)
            bit //= 2
    return total, exchange(total, 1, size)


def collect(me, masks, pieces, nodes):
    if nodes is None:
        return pieces[0]
    rows = pieces[0].shape[0]
    for mask, piece in zip(masks, pieces):
        blocks = piece.shape[0]
        start = (me ^ mask) * blocks
        for i in range(blocks):
            nodes[start + i] = piece[i]
    return nodes


def panel_product(cols, counts, vals, nodes, panel):
    used = counts[panel]
    side = vals.shape[2]

    def product(b):
        return jnp.dot(
            vals[panel, b], nodes[cols[panel, b]], preferred_element_type=jnp.float32
        )

    def many(step, total):
        for j in range(GROUP):
            total = total + product(step * GROUP + j)
        return total

    full = used // GROUP
    total = lax.fori_loop(0, full, many, jnp.zeros((side, nodes.shape[2]), jnp.float32))
    return lax.fori_loop(full * GROUP, used, lambda b, t: t + product(b), total)


def split(x):
    high = x.astype(jnp.bfloat16)
    return high, (x - high.astype(jnp.float32)).astype(jnp.bfloat16)


def dot(a, b, dims):
    return lax.dot_general(a, b, (dims, ((), ())), preferred_element_type=jnp.float32)


def forward_kernel(masks, *refs):
    n = len(masks)
    cols, counts = refs[:2]
    pieces = refs[2 : 2 + n]
    vals, weight, out_grad = refs[2 + n : 5 + n]
    hidden, edge, keep, send = refs[5 + n : 9 + n]
    wsum = refs[9 + n]
    me = lax.axis_index("row")
    nodes = collect(me, masks, pieces, refs[10 + n] if n > 1 else None)
    panels, _, side, _ = vals.shape
    half = keep.shape[0]
    w = weight[...]
    for panel in range(panels):
        rows = pl.ds(panel * side, side)
        agg = panel_product(cols, counts, vals, nodes, panel)
        agg_h, agg_l = split(agg)
        z = dot(agg_h, w, ((1,), (0,))) + dot(agg_l, w, ((1,), (0,)))
        zz = z * z
        t = jnp.tanh(z * (GELU_C + (GELU_C * GELU_A) * zz))
        half_up = 0.5 + 0.5 * t
        hidden[rows, :] = (z * half_up).astype(jnp.bfloat16)
        slope = half_up + (0.5 * z) * (1.0 - t * t) * (GELU_C + (3.0 * GELU_C * GELU_A) * zz)
        dz = out_grad[rows, :].astype(jnp.float32) * slope
        dz_h, dz_l = split(dz)
        edge[panel] = (dot(dz_h, w, ((1,), (1,))) + dot(dz_l, w, ((1,), (1,)))).astype(jnp.bfloat16)
        part = (
            dot(agg_h, dz_h, ((0,), (0,)))
            + dot(agg_l, dz_h, ((0,), (0,)))
            + dot(agg_h, dz_l, ((0,), (0,)))
        )
        wsum[...] = part if panel == 0 else wsum[...] + part
    core = me % 2
    keep[...] = wsum[pl.ds(pl.multiple_of(core * half, half), half), :]
    send[...] = wsum[pl.ds(pl.multiple_of((1 - core) * half, half), half), :]


def backward_kernel(masks, *refs):
    n = len(masks)
    cols, counts = refs[:2]
    pieces = refs[2 : 2 + n]
    vals, own, other = refs[2 + n : 5 + n]
    feat, weight_grad = refs[5 + n : 7 + n]
    me = lax.axis_index("row")
    half = own.shape[0]
    core = me % 2
    weight_grad[pl.ds(pl.multiple_of(core * half, half), half), :] = own[...]
    weight_grad[pl.ds(pl.multiple_of((1 - core) * half, half), half), :] = other[...]
    nodes = collect(me, masks, pieces, refs[7 + n] if n > 1 else None)
    panels, _, side, _ = vals.shape
    for panel in range(panels):
        rows = pl.ds(panel * side, side)
        feat[rows, :] = panel_product(cols, counts, vals, nodes, panel).astype(jnp.bfloat16)


def body(features, weight, block_cols, block_counts, block_vals, out_grad):
    size = lax.axis_size("row")
    panels, _, side, _ = block_vals.shape
    rows, width = features.shape
    hidden_width = weight.shape[1]
    node_blocks = size * panels
    features_in = features.reshape(panels, side, width)
    vals, out_grad, weight, own_rows = stage(block_vals, out_grad, weight, features_in)

    def gathered(x, own, staged=None):
        held = gather_rows(x, own, size, staged)
        scratch = []
        if len(held) > 1:
            scratch = [pltpu.VMEM((node_blocks, side, width), jnp.bfloat16)]
        return held, tuple(m for m, _ in held), [in_vmem(a) for _, a in held], scratch

    held, masks, pieces, scratch = gathered(features_in, own_rows, own_rows)
    hidden, edge, keep, send = pl.pallas_call(
        lambda *refs: forward_kernel(masks, *refs),
        name="forward",
        compiler_params=PARAMS,
        out_shape=(
            jax.ShapeDtypeStruct((rows, hidden_width), jnp.bfloat16),
            jax.ShapeDtypeStruct((panels, side, width), jnp.bfloat16),
            jax.ShapeDtypeStruct((width // 2, hidden_width), jnp.float32),
            jax.ShapeDtypeStruct((width // 2, hidden_width), jnp.float32),
        ),
        in_specs=[SMEM] * 2 + [VMEM] * (len(pieces) + 3),
        out_specs=(VMEM,) * 4,
        scratch_shapes=[pltpu.VMEM((width, hidden_width), jnp.float32)] + scratch,
    )(block_cols, block_counts, *pieces, in_vmem(vals), in_vmem(weight), in_vmem(out_grad))

    held, masks, pieces, scratch = gathered(edge, edge)
    own, other = row_sum(keep, send, held, size)
    feat_grad, weight_grad = pl.pallas_call(
        lambda *refs: backward_kernel(masks, *refs),
        name="backward",
        compiler_params=PARAMS,
        out_shape=(
            jax.ShapeDtypeStruct((rows, width), jnp.bfloat16),
            jax.ShapeDtypeStruct((width, hidden_width), jnp.float32),
        ),
        in_specs=[SMEM] * 2 + [VMEM] * (len(pieces) + 3),
        out_specs=(VMEM, VMEM),
        scratch_shapes=scratch,
    )(block_cols, block_counts, *pieces, in_vmem(vals), in_vmem(own), in_vmem(other))
    return hidden, feat_grad, weight_grad


def solution(mesh):
    in_specs = (
        P(("groups", "row"), None),
        P(),
        P(("groups", "row"), None),
        P(("groups", "row")),
        P(("groups", "row"), None, None, None),
        P(("groups", "row"), None),
    )
    out_specs = (P(("groups", "row"), None), P(("groups", "row"), None), P("groups", None))
    return jax.shard_map(body, mesh=mesh, in_specs=in_specs, out_specs=out_specs, check_vma=False)
```

```python
import jax
import jax.numpy as jnp
from jax import lax
from jax.experimental import pallas as pl
from jax.experimental.pallas import tpu as pltpu
from jax.sharding import PartitionSpec as P

GROUP = 2
GELU_C = 0.7978845608028654
GELU_A = 0.044715
PARAMS = pltpu.CompilerParams(vmem_limit_bytes=12 * 2**20)
SMEM = pl.BlockSpec(memory_space=pltpu.SMEM)
VMEM = pl.BlockSpec(memory_space=pltpu.VMEM)


def in_vmem(x):
    return pltpu.with_memory_space_constraint(x, pltpu.VMEM)


def stage(*arrays):
    n = len(arrays)

    def kernel(*refs):
        sems = refs[2 * n]
        copies = [
            pltpu.make_async_copy(refs[i], refs[n + i], sems.at[i]) for i in range(n)
        ]
        for c in copies:
            c.start()
        for c in copies:
            c.wait()

    return pl.pallas_call(
        kernel,
        name="stage",
        compiler_params=PARAMS,
        out_shape=tuple(pltpu.VMEM(a.shape, a.dtype) for a in arrays),
        in_specs=[pl.BlockSpec(memory_space=pltpu.HBM)] * n,
        out_specs=(VMEM,) * n,
        scratch_shapes=[pltpu.SemaphoreType.DMA((n,))],
    )(*(pltpu.with_memory_space_constraint(a, pltpu.HBM) for a in arrays))


def exchange(x, bit, size):
    return lax.ppermute(x, "row", [(i, i ^ bit) for i in range(size)])


def after(x, *others):
    return lax.optimization_barrier((x, *others))[0]


def gather_rows(x, own, size, staged=None):
    if size != 16:
        return [(None, lax.all_gather(x, "row", axis=0, tiled=True))]
    held = {0: x}
    held[8] = exchange(x, 8, size)
    held[4] = exchange(x, 4, size)
    far = held[8] if staged is None else after(held[8], staged)
    held[12] = exchange(far, 4, size)
    held[2] = exchange(x, 2, size)
    held[6] = exchange(held[2], 4, size)
    held[10] = exchange(held[8], 2, size)
    held[14] = exchange(held[12], 2, size)
    for mask in (0, 2, 4, 6, 8, 10, 12, 14):
        held[mask ^ 1] = exchange(held[mask], 1, size)
    held[0] = own
    return sorted(held.items())


def row_sum(keep, send, held, size):
    held = dict(held)
    total = keep + exchange(send, 1, size)
    if size == 16:
        total = total + exchange(total, 8, size)
        total = total + exchange(after(total, held[8]), 4, size)
        total = total + exchange(after(total, held[12]), 2, size)
    else:
        bit = size // 2
        while bit > 1:
            total = total + exchange(total, bit, size)
            bit //= 2
    return total, exchange(total, 1, size)


def collect(me, masks, pieces, nodes):
    if nodes is None:
        return pieces[0]
    rows = pieces[0].shape[0]
    for mask, piece in zip(masks, pieces):
        blocks = piece.shape[0]
        start = (me ^ mask) * blocks
        for i in range(blocks):
            nodes[start + i] = piece[i]
    return nodes


def panel_product(cols, counts, vals, nodes, panel):
    used = counts[panel]
    slots, side = vals.shape[1:3]
    none = jnp.zeros((side, side), vals.dtype)
    total = None
    for b in range(0, slots, GROUP):
        group = range(b, b + GROUP)
        part = jnp.dot(
            jnp.concatenate([jnp.where(i < used, vals[panel, i], none) for i in group], 1),
            jnp.concatenate([nodes[cols[panel, i]] for i in group], 0),
            preferred_element_type=jnp.float32,
        )
        total = part if total is None else total + part
    return total

def split(x):
    high = x.astype(jnp.bfloat16)
    return high, (x - high.astype(jnp.float32)).astype(jnp.bfloat16)


def dot(a, b, dims):
    return lax.dot_general(a, b, (dims, ((), ())), preferred_element_type=jnp.float32)


def forward_kernel(masks, *refs):
    n = len(masks)
    cols, counts = refs[:2]
    pieces = refs[2 : 2 + n]
    vals, weight, out_grad = refs[2 + n : 5 + n]
    hidden, edge, keep, send = refs[5 + n : 9 + n]
    wsum = refs[9 + n]
    me = lax.axis_index("row")
    nodes = collect(me, masks, pieces, refs[10 + n] if n > 1 else None)
    panels, _, side, _ = vals.shape
    half = keep.shape[0]
    w = weight[...]
    ww = jnp.concatenate([w, w], 0)
    for panel in range(panels):
        rows = pl.ds(panel * side, side)
        agg = panel_product(cols, counts, vals, nodes, panel)
        agg_h, agg_l = split(agg)
        z = dot(jnp.concatenate([agg_h, agg_l], 1), ww, ((1,), (0,)))
        zz = z * z
        t = jnp.tanh(z * (GELU_C + (GELU_C * GELU_A) * zz))
        half_up = 0.5 + 0.5 * t
        hidden[rows, :] = (z * half_up).astype(jnp.bfloat16)
        slope = half_up + (0.5 * z) * (1.0 - t * t) * (GELU_C + (3.0 * GELU_C * GELU_A) * zz)
        dz = out_grad[rows, :].astype(jnp.float32) * slope
        dz_h, dz_l = split(dz)
        edge[panel] = (dot(dz_h, w, ((1,), (1,))) + dot(dz_l, w, ((1,), (1,)))).astype(jnp.bfloat16)
        part = dot(
            jnp.concatenate([agg_h, agg_l, agg_h], 0),
            jnp.concatenate([dz_h, dz_h, dz_l], 0),
            ((0,), (0,)),
        )
        wsum[...] = part if panel == 0 else wsum[...] + part
    core = me % 2
    keep[...] = wsum[pl.ds(pl.multiple_of(core * half, half), half), :]
    send[...] = wsum[pl.ds(pl.multiple_of((1 - core) * half, half), half), :]


def backward_kernel(masks, *refs):
    n = len(masks)
    cols, counts = refs[:2]
    pieces = refs[2 : 2 + n]
    vals, own, other = refs[2 + n : 5 + n]
    feat, weight_grad = refs[5 + n : 7 + n]
    me = lax.axis_index("row")
    half = own.shape[0]
    core = me % 2
    weight_grad[pl.ds(pl.multiple_of(core * half, half), half), :] = own[...]
    weight_grad[pl.ds(pl.multiple_of((1 - core) * half, half), half), :] = other[...]
    nodes = collect(me, masks, pieces, refs[7 + n] if n > 1 else None)
    panels, _, side, _ = vals.shape
    for panel in range(panels):
        rows = pl.ds(panel * side, side)
        feat[rows, :] = panel_product(cols, counts, vals, nodes, panel).astype(jnp.bfloat16)


def body(features, weight, block_cols, block_counts, block_vals, out_grad):
    size = lax.axis_size("row")
    panels, _, side, _ = block_vals.shape
    rows, width = features.shape
    hidden_width = weight.shape[1]
    node_blocks = size * panels
    features_in = features.reshape(panels, side, width)
    vals, out_grad, weight, own_rows = stage(block_vals, out_grad, weight, features_in)

    def gathered(x, own, staged=None):
        held = gather_rows(x, own, size, staged)
        scratch = []
        if len(held) > 1:
            scratch = [pltpu.VMEM((node_blocks, side, width), jnp.bfloat16)]
        return held, tuple(m for m, _ in held), [in_vmem(a) for _, a in held], scratch

    held, masks, pieces, scratch = gathered(features_in, own_rows, own_rows)
    hidden, edge, keep, send = pl.pallas_call(
        lambda *refs: forward_kernel(masks, *refs),
        name="forward",
        compiler_params=PARAMS,
        out_shape=(
            pltpu.VMEM((rows, hidden_width), jnp.bfloat16),
            pltpu.VMEM((panels, side, width), jnp.bfloat16),
            pltpu.VMEM((width // 2, hidden_width), jnp.float32),
            pltpu.VMEM((width // 2, hidden_width), jnp.float32),
        ),
        in_specs=[SMEM] * 2 + [VMEM] * (len(pieces) + 3),
        out_specs=(VMEM,) * 4,
        scratch_shapes=[pltpu.VMEM((width, hidden_width), jnp.float32)] + scratch,
    )(block_cols, block_counts, *pieces, in_vmem(vals), in_vmem(weight), in_vmem(out_grad))

    held, masks, pieces, scratch = gathered(edge, edge)
    own, other = row_sum(keep, send, held, size)
    feat_grad, weight_grad = pl.pallas_call(
        lambda *refs: backward_kernel(masks, *refs),
        name="backward",
        compiler_params=PARAMS,
        out_shape=(
            jax.ShapeDtypeStruct((rows, width), jnp.bfloat16),
            jax.ShapeDtypeStruct((width, hidden_width), jnp.float32),
        ),
        in_specs=[SMEM] * 2 + [VMEM] * (len(pieces) + 3),
        out_specs=(VMEM, VMEM),
        scratch_shapes=scratch,
    )(block_cols, block_counts, *pieces, in_vmem(vals), in_vmem(own), in_vmem(other))
    return hidden, feat_grad, weight_grad


def solution(mesh):
    in_specs = (
        P(("groups", "row"), None),
        P(),
        P(("groups", "row"), None),
        P(("groups", "row")),
        P(("groups", "row"), None, None, None),
        P(("groups", "row"), None),
    )
    out_specs = (P(("groups", "row"), None), P(("groups", "row"), None), P("groups", None))
    return jax.shard_map(body, mesh=mesh, in_specs=in_specs, out_specs=out_specs, check_vma=False)
```

```python
import jax
import jax.numpy as jnp
from jax import lax
from jax.experimental import pallas as pl
from jax.experimental.pallas import tpu as pltpu
from jax.sharding import PartitionSpec as P

GROUP = 2
GELU_C = 0.7978845608028654
GELU_A = 0.044715
PARAMS = pltpu.CompilerParams(vmem_limit_bytes=12 * 2**20)
SMEM = pl.BlockSpec(memory_space=pltpu.SMEM)
VMEM = pl.BlockSpec(memory_space=pltpu.VMEM)
HBM = pl.BlockSpec(memory_space=pltpu.HBM)


def in_vmem(x):
    return pltpu.with_memory_space_constraint(x, pltpu.VMEM)


def in_hbm(x):
    return pltpu.with_memory_space_constraint(x, pltpu.HBM)


def in_smem(x):
    return pltpu.with_memory_space_constraint(x, pltpu.SMEM)


def run(copies):
    for c in copies:
        c.start()
    for c in copies:
        c.wait()


def stage_kernel(cols, counts, vals, *refs):
    n = (len(refs) - 3) // 2
    plain, refs = refs[:n], refs[n:]
    cols_out, vals_out = refs[:2]
    plain_out = refs[2 : 2 + n]
    counts_in, sems = refs[2 + n :]
    pairs = [(counts, counts_in), (cols, cols_out), (vals, vals_out), *zip(plain, plain_out)]
    run([pltpu.make_async_copy(i, o, sems.at[k]) for k, (i, o) in enumerate(pairs)])
    panels, slots = vals_out.shape[:2]
    for panel in range(panels):
        for slot in range(slots):

            @pl.when(slot >= counts_in[panel])
            def _():
                vals_out[panel, slot] = jnp.zeros(vals_out.shape[2:], vals_out.dtype)


def stage(cols, counts, vals, *plain):
    n = len(plain)
    return pl.pallas_call(
        stage_kernel,
        name="stage",
        compiler_params=PARAMS,
        out_shape=(
            pltpu.SMEM(cols.shape, cols.dtype),
            *(pltpu.VMEM(a.shape, a.dtype) for a in (vals, *plain)),
        ),
        in_specs=[HBM] * (3 + n),
        out_specs=(SMEM,) + (VMEM,) * (1 + n),
        scratch_shapes=[
            pltpu.SMEM(counts.shape, counts.dtype),
            pltpu.SemaphoreType.DMA((3 + n,)),
        ],
    )(*(in_hbm(a) for a in (cols, counts, vals, *plain)))


def unstage_kernel(x, out, sem):
    run([pltpu.make_async_copy(x, out, sem)])


def unstage(x):
    return pl.pallas_call(
        unstage_kernel,
        name="unstage",
        compiler_params=PARAMS,
        out_shape=jax.ShapeDtypeStruct(x.shape, x.dtype),
        in_specs=[VMEM],
        out_specs=HBM,
        scratch_shapes=[pltpu.SemaphoreType.DMA],
    )(in_vmem(x))


def exchange(x, bit, size):
    return lax.ppermute(x, "row", [(i, i ^ bit) for i in range(size)])


def after(x, *others):
    return lax.optimization_barrier((x, *others))[0]


def gather_rows(x, own, size, staged=None):
    if size != 16:
        return [(None, lax.all_gather(x, "row", axis=0, tiled=True))]
    held = {0: x}
    held[8] = exchange(x, 8, size)
    held[4] = exchange(x, 4, size)
    far = held[8] if staged is None else after(held[8], staged)
    held[12] = exchange(far, 4, size)
    held[2] = exchange(x, 2, size)
    held[6] = exchange(held[2], 4, size)
    held[10] = exchange(held[8], 2, size)
    held[14] = exchange(held[12], 2, size)
    for mask in (0, 2, 4, 6, 8, 10, 12, 14):
        held[mask ^ 1] = exchange(held[mask], 1, size)
    held[0] = own
    return sorted(held.items())


def row_sum(keep, send, held, size):
    held = dict(held)
    total = keep + exchange(send, 1, size)
    if size == 16:
        total = total + exchange(total, 8, size)
        total = total + exchange(after(total, held[8]), 4, size)
        total = total + exchange(after(total, held[12]), 2, size)
    else:
        bit = size // 2
        while bit > 1:
            total = total + exchange(total, bit, size)
            bit //= 2
    return total, exchange(total, 1, size)


def collect(me, masks, pieces, nodes):
    if nodes is None:
        return pieces[0]
    rows = pieces[0].shape[0]
    for mask, piece in zip(masks, pieces):
        blocks = piece.shape[0]
        start = (me ^ mask) * blocks
        for i in range(blocks):
            nodes[start + i] = piece[i]
    return nodes


def panel_product(cols, vals, nodes, panel):
    total = None
    for b in range(0, vals.shape[1], GROUP):
        group = range(b, b + GROUP)
        part = jnp.dot(
            jnp.concatenate([vals[panel, i] for i in group], 1),
            jnp.concatenate([nodes[cols[panel, i]] for i in group], 0),
            preferred_element_type=jnp.float32,
        )
        total = part if total is None else total + part
    return total


def split(x):
    high = x.astype(jnp.bfloat16)
    return high, (x - high.astype(jnp.float32)).astype(jnp.bfloat16)


def dot(a, b, dims):
    return lax.dot_general(a, b, (dims, ((), ())), preferred_element_type=jnp.float32)


def forward_kernel(masks, *refs):
    n = len(masks)
    cols = refs[0]
    pieces = refs[1 : 1 + n]
    vals, weight, out_grad = refs[1 + n : 4 + n]
    hidden, edge, keep, send = refs[4 + n : 8 + n]
    wsum = refs[8 + n]
    me = lax.axis_index("row")
    nodes = collect(me, masks, pieces, refs[9 + n] if n > 1 else None)
    panels, _, side, _ = vals.shape
    half = keep.shape[0]
    w = weight[...]
    ww = jnp.concatenate([w, w], 0)
    for panel in range(panels):
        rows = pl.ds(panel * side, side)
        agg = panel_product(cols, vals, nodes, panel)
        agg_h, agg_l = split(agg)
        z = dot(jnp.concatenate([agg_h, agg_l], 1), ww, ((1,), (0,)))
        zz = z * z
        t = jnp.tanh(z * (GELU_C + (GELU_C * GELU_A) * zz))
        half_up = 0.5 + 0.5 * t
        hidden[rows, :] = (z * half_up).astype(jnp.bfloat16)
        slope = half_up + (0.5 * z) * (1.0 - t * t) * (GELU_C + (3.0 * GELU_C * GELU_A) * zz)
        dz = out_grad[rows, :].astype(jnp.float32) * slope
        dz_h, dz_l = split(dz)
        edge[panel] = (dot(dz_h, w, ((1,), (1,))) + dot(dz_l, w, ((1,), (1,)))).astype(jnp.bfloat16)
        part = dot(
            jnp.concatenate([agg_h, agg_l, agg_h], 0),
            jnp.concatenate([dz_h, dz_h, dz_l], 0),
            ((0,), (0,)),
        )
        wsum[...] = part if panel == 0 else wsum[...] + part
    core = me % 2
    keep[...] = wsum[pl.ds(pl.multiple_of(core * half, half), half), :]
    send[...] = wsum[pl.ds(pl.multiple_of((1 - core) * half, half), half), :]


def backward_kernel(masks, *refs):
    n = len(masks)
    cols = refs[0]
    pieces = refs[1 : 1 + n]
    vals, own, other = refs[1 + n : 4 + n]
    feat, weight_grad, rows, sems = refs[4 + n : 8 + n]
    me = lax.axis_index("row")
    panels, _, side, _ = vals.shape
    half = own.shape[0]
    copies = []

    def send(source, target):
        copies.append(pltpu.make_async_copy(source, target, sems.at[len(copies)]))
        copies[-1].start()

    core = me % 2
    send(own, weight_grad.at[pl.ds(pl.multiple_of(core * half, half), half)])
    send(other, weight_grad.at[pl.ds(pl.multiple_of((1 - core) * half, half), half)])
    nodes = collect(me, masks, pieces, refs[8 + n] if n > 1 else None)
    for panel in range(panels):
        here = pl.ds(panel * side, side)
        rows[here, :] = panel_product(cols, vals, nodes, panel).astype(jnp.bfloat16)
        send(rows.at[here], feat.at[here])
    for c in copies:
        c.wait()


def body(features, weight, block_cols, block_counts, block_vals, out_grad):
    size = lax.axis_size("row")
    panels, _, side, _ = block_vals.shape
    rows, width = features.shape
    hidden_width = weight.shape[1]
    node_blocks = size * panels
    features_in = features.reshape(panels, side, width)
    cols, vals, out_grad, weight, own_rows = stage(
        block_cols, block_counts, block_vals, out_grad, weight, features_in
    )
    cols, vals = in_smem(cols), in_vmem(vals)

    def gathered(x, own, staged=None):
        held = gather_rows(x, own, size, staged)
        scratch = []
        if len(held) > 1:
            scratch = [pltpu.VMEM((node_blocks, side, width), jnp.bfloat16)]
        return held, tuple(m for m, _ in held), [in_vmem(a) for _, a in held], scratch

    held, masks, pieces, scratch = gathered(features_in, own_rows, own_rows)
    hidden, edge, keep, send = pl.pallas_call(
        lambda *refs: forward_kernel(masks, *refs),
        name="forward",
        compiler_params=PARAMS,
        out_shape=(
            pltpu.VMEM((rows, hidden_width), jnp.bfloat16),
            pltpu.VMEM((panels, side, width), jnp.bfloat16),
            pltpu.VMEM((width // 2, hidden_width), jnp.float32),
            pltpu.VMEM((width // 2, hidden_width), jnp.float32),
        ),
        in_specs=[SMEM] + [VMEM] * (len(pieces) + 3),
        out_specs=(VMEM,) * 4,
        scratch_shapes=[pltpu.VMEM((width, hidden_width), jnp.float32)] + scratch,
    )(cols, *pieces, vals, in_vmem(weight), in_vmem(out_grad))

    hidden = unstage(hidden)
    held, masks, pieces, scratch = gathered(edge, edge, hidden)
    own, other = row_sum(keep, send, held, size)
    feat_grad, weight_grad = pl.pallas_call(
        lambda *refs: backward_kernel(masks, *refs),
        name="backward",
        compiler_params=PARAMS,
        out_shape=(
            jax.ShapeDtypeStruct((rows, width), jnp.bfloat16),
            jax.ShapeDtypeStruct((width, hidden_width), jnp.float32),
        ),
        in_specs=[SMEM] + [VMEM] * (len(pieces) + 3),
        out_specs=(HBM, HBM),
        scratch_shapes=[
            pltpu.VMEM((rows, width), jnp.bfloat16),
            pltpu.SemaphoreType.DMA((panels + 2,)),
        ]
        + scratch,
    )(cols, *pieces, vals, in_vmem(own), in_vmem(other))
    return hidden, feat_grad, weight_grad


def solution(mesh):
    in_specs = (
        P(("groups", "row"), None),
        P(),
        P(("groups", "row"), None),
        P(("groups", "row")),
        P(("groups", "row"), None, None, None),
        P(("groups", "row"), None),
    )
    out_specs = (P(("groups", "row"), None), P(("groups", "row"), None), P("groups", None))
    return jax.shard_map(body, mesh=mesh, in_specs=in_specs, out_specs=out_specs, check_vma=False)
```

```python
import jax
import jax.numpy as jnp
from jax import lax
from jax.experimental import pallas as pl
from jax.experimental.pallas import tpu as pltpu
from jax.sharding import PartitionSpec as P

GROUP = 2
GELU_C = 0.7978845608028654
GELU_A = 0.044715
PARAMS = pltpu.CompilerParams(vmem_limit_bytes=12 * 2**20)
SMEM = pl.BlockSpec(memory_space=pltpu.SMEM)
VMEM = pl.BlockSpec(memory_space=pltpu.VMEM)
HBM = pl.BlockSpec(memory_space=pltpu.HBM)


def in_vmem(x):
    return pltpu.with_memory_space_constraint(x, pltpu.VMEM)


def in_hbm(x):
    return pltpu.with_memory_space_constraint(x, pltpu.HBM)


def in_smem(x):
    return pltpu.with_memory_space_constraint(x, pltpu.SMEM)


def run(copies):
    for c in copies:
        c.start()
    for c in copies:
        c.wait()


def stage_kernel(cols, counts, vals, *refs):
    n = (len(refs) - 3) // 2
    plain, refs = refs[:n], refs[n:]
    cols_out, vals_out = refs[:2]
    plain_out = refs[2 : 2 + n]
    counts_in, sems = refs[2 + n :]
    pairs = [(counts, counts_in), (cols, cols_out), (vals, vals_out), *zip(plain, plain_out)]
    run([pltpu.make_async_copy(i, o, sems.at[k]) for k, (i, o) in enumerate(pairs)])
    panels, slots = vals_out.shape[:2]
    for panel in range(panels):

        def clear(slot, carry):
            vals_out[panel, slot] = jnp.zeros(vals_out.shape[2:], vals_out.dtype)
            return carry

        lax.fori_loop(counts_in[panel], slots, clear, 0)


def stage(cols, counts, vals, *plain):
    n = len(plain)
    return pl.pallas_call(
        stage_kernel,
        name="stage",
        compiler_params=PARAMS,
        out_shape=(
            pltpu.SMEM(cols.shape, cols.dtype),
            *(pltpu.VMEM(a.shape, a.dtype) for a in (vals, *plain)),
        ),
        in_specs=[HBM] * (3 + n),
        out_specs=(SMEM,) + (VMEM,) * (1 + n),
        scratch_shapes=[
            pltpu.SMEM(counts.shape, counts.dtype),
            pltpu.SemaphoreType.DMA((3 + n,)),
        ],
    )(*(in_hbm(a) for a in (cols, counts, vals, *plain)))


def unstage_kernel(x, out, sem):
    run([pltpu.make_async_copy(x, out, sem)])


def unstage(x):
    return pl.pallas_call(
        unstage_kernel,
        name="unstage",
        compiler_params=PARAMS,
        out_shape=jax.ShapeDtypeStruct(x.shape, x.dtype),
        in_specs=[VMEM],
        out_specs=HBM,
        scratch_shapes=[pltpu.SemaphoreType.DMA],
    )(in_vmem(x))


def exchange(x, bit, size):
    return lax.ppermute(x, "row", [(i, i ^ bit) for i in range(size)])


def after(x, *others):
    return lax.optimization_barrier((x, *others))[0]


def pack_kernel(*refs):
    out, start = refs[-1], 0
    for r in refs[:-1]:
        out[pl.ds(start, r.shape[0])] = r[...]
        start += r.shape[0]


def pack(arrays):
    if len(arrays) == 1:
        return arrays[0]
    first = arrays[0]
    total = sum(a.shape[0] for a in arrays)
    return pl.pallas_call(
        pack_kernel,
        name="pack",
        compiler_params=PARAMS,
        out_shape=pltpu.VMEM((total, *first.shape[1:]), first.dtype),
        in_specs=[VMEM] * len(arrays),
        out_specs=VMEM,
    )(*(in_vmem(a) for a in arrays))


CORE_GROUPS = ((0, 2, 4, 8), (6, 10), (12, 14))
SUM_BITS = (2, 8, 4)


def row_sum(keep, send, size, bits):
    total = keep + exchange(send, 1, size)
    for bit in bits:
        total = total + exchange(total, bit, size)
    return total


def gather_rows(x, own, size, staged, halves=None):
    sums = None
    if size != 16:
        if halves is not None:
            bits = [1 << k for k in range(1, (size - 1).bit_length())]
            total = row_sum(*halves, size, bits)
            sums = total, exchange(total, 1, size)
        return [((None,), lax.all_gather(x, "row", axis=0, tiled=True))], sums

    def step(value, k):
        return value if halves is None else after(value, totals[k])

    def advance():
        if halves is not None:
            bit = SUM_BITS[len(totals) - 1]
            totals.append(totals[-1] + exchange(totals[-1], bit, size))

    held = {8: exchange(x, 8, size), 4: exchange(x, 4, size)}
    totals = [] if halves is None else [halves[0] + exchange(halves[1], 1, size)]
    held[12] = exchange(step(after(held[8], staged), 0), 4, size)
    held[2] = exchange(x, 2, size)
    held[6] = exchange(held[2], 4, size)
    advance()
    held[10] = exchange(step(held[8], 1), 2, size)
    advance()
    held[14] = exchange(step(held[12], 2), 2, size)
    advance()
    if halves is not None:
        sums = totals[-1], exchange(totals[-1], 1, size)
    held[0] = own
    pieces = [((mask,), held[mask]) for mask in sorted(held)]
    for group in CORE_GROUPS:
        arrays = [held[mask] for mask in group]
        if group is CORE_GROUPS[-1]:
            arrays[0] = step(arrays[0], 3)
        pieces.append((tuple(mask ^ 1 for mask in group), exchange(pack(arrays), 1, size)))
    return pieces, sums


def collect(me, masks, pieces, nodes):
    if nodes is None:
        return pieces[0]
    for each, piece in zip(masks, pieces):
        blocks = piece.shape[0] // len(each)
        for k, mask in enumerate(each):
            start = (me ^ mask) * blocks
            for i in range(blocks):
                nodes[start + i] = piece[k * blocks + i]
    return nodes


def panel_product(cols, vals, nodes, panel):
    total = None
    for b in range(0, vals.shape[1], GROUP):
        group = range(b, b + GROUP)
        part = jnp.dot(
            jnp.concatenate([vals[panel, i] for i in group], 1),
            jnp.concatenate([nodes[cols[panel, i]] for i in group], 0),
            preferred_element_type=jnp.float32,
        )
        total = part if total is None else total + part
    return total


def split(x):
    high = x.astype(jnp.bfloat16)
    return high, (x - high.astype(jnp.float32)).astype(jnp.bfloat16)


def dot(a, b, dims):
    return lax.dot_general(a, b, (dims, ((), ())), preferred_element_type=jnp.float32)


def forward_kernel(masks, *refs):
    n = len(masks)
    cols = refs[0]
    pieces = refs[1 : 1 + n]
    vals, weight, out_grad = refs[1 + n : 4 + n]
    hidden, edge, keep, send = refs[4 + n : 8 + n]
    wsum = refs[8 + n]
    me = lax.axis_index("row")
    nodes = collect(me, masks, pieces, refs[9 + n] if n > 1 else None)
    panels, _, side, _ = vals.shape
    half = keep.shape[0]
    w = weight[...]
    ww = jnp.concatenate([w, w], 0)
    for panel in range(panels):
        rows = pl.ds(panel * side, side)
        agg = panel_product(cols, vals, nodes, panel)
        agg_h, agg_l = split(agg)
        z = dot(jnp.concatenate([agg_h, agg_l], 1), ww, ((1,), (0,)))
        zz = z * z
        t = jnp.tanh(z * (GELU_C + (GELU_C * GELU_A) * zz))
        half_up = 0.5 + 0.5 * t
        hidden[rows, :] = (z * half_up).astype(jnp.bfloat16)
        slope = half_up + (0.5 * z) * (1.0 - t * t) * (GELU_C + (3.0 * GELU_C * GELU_A) * zz)
        dz = out_grad[rows, :].astype(jnp.float32) * slope
        dz_h, dz_l = split(dz)
        edge[panel] = (dot(dz_h, w, ((1,), (1,))) + dot(dz_l, w, ((1,), (1,)))).astype(jnp.bfloat16)
        part = dot(
            jnp.concatenate([agg_h, agg_l, agg_h], 0),
            jnp.concatenate([dz_h, dz_h, dz_l], 0),
            ((0,), (0,)),
        )
        wsum[...] = part if panel == 0 else wsum[...] + part
    core = me % 2
    keep[...] = wsum[pl.ds(pl.multiple_of(core * half, half), half), :]
    send[...] = wsum[pl.ds(pl.multiple_of((1 - core) * half, half), half), :]


def backward_kernel(masks, *refs):
    n = len(masks)
    cols = refs[0]
    pieces = refs[1 : 1 + n]
    vals, own, other = refs[1 + n : 4 + n]
    feat, weight_grad, rows, sems = refs[4 + n : 8 + n]
    me = lax.axis_index("row")
    panels, _, side, _ = vals.shape
    half = own.shape[0]
    copies = []

    def send(source, target):
        copies.append(pltpu.make_async_copy(source, target, sems.at[len(copies)]))
        copies[-1].start()

    core = me % 2
    send(own, weight_grad.at[pl.ds(pl.multiple_of(core * half, half), half)])
    send(other, weight_grad.at[pl.ds(pl.multiple_of((1 - core) * half, half), half)])
    nodes = collect(me, masks, pieces, refs[8 + n] if n > 1 else None)
    for panel in range(panels):
        here = pl.ds(panel * side, side)
        rows[here, :] = panel_product(cols, vals, nodes, panel).astype(jnp.bfloat16)
        send(rows.at[here], feat.at[here])
    for c in copies:
        c.wait()


def body(features, weight, block_cols, block_counts, block_vals, out_grad):
    size = lax.axis_size("row")
    panels, _, side, _ = block_vals.shape
    rows, width = features.shape
    hidden_width = weight.shape[1]
    node_blocks = size * panels
    features_in = features.reshape(panels, side, width)
    cols, vals, out_grad, weight, own_rows = stage(
        block_cols, block_counts, block_vals, out_grad, weight, features_in
    )
    cols, vals = in_smem(cols), in_vmem(vals)

    def gathered(*arrays):
        pieces, sums = gather_rows(*arrays)
        scratch = []
        if len(pieces) > 1:
            scratch = [pltpu.VMEM((node_blocks, side, width), jnp.bfloat16)]
        return sums, tuple(m for m, _ in pieces), [in_vmem(a) for _, a in pieces], scratch

    _, masks, pieces, scratch = gathered(features_in, own_rows, size, own_rows)
    hidden, edge, keep, send = pl.pallas_call(
        lambda *refs: forward_kernel(masks, *refs),
        name="forward",
        compiler_params=PARAMS,
        out_shape=(
            pltpu.VMEM((rows, hidden_width), jnp.bfloat16),
            pltpu.VMEM((panels, side, width), jnp.bfloat16),
            pltpu.VMEM((width // 2, hidden_width), jnp.float32),
            pltpu.VMEM((width // 2, hidden_width), jnp.float32),
        ),
        in_specs=[SMEM] + [VMEM] * (len(pieces) + 3),
        out_specs=(VMEM,) * 4,
        scratch_shapes=[pltpu.VMEM((width, hidden_width), jnp.float32)] + scratch,
    )(cols, *pieces, vals, in_vmem(weight), in_vmem(out_grad))

    hidden = unstage(hidden)
    (own, other), masks, pieces, scratch = gathered(edge, edge, size, hidden, (keep, send))
    feat_grad, weight_grad = pl.pallas_call(
        lambda *refs: backward_kernel(masks, *refs),
        name="backward",
        compiler_params=PARAMS,
        out_shape=(
            jax.ShapeDtypeStruct((rows, width), jnp.bfloat16),
            jax.ShapeDtypeStruct((width, hidden_width), jnp.float32),
        ),
        in_specs=[SMEM] + [VMEM] * (len(pieces) + 3),
        out_specs=(HBM, HBM),
        scratch_shapes=[
            pltpu.VMEM((rows, width), jnp.bfloat16),
            pltpu.SemaphoreType.DMA((panels + 2,)),
        ]
        + scratch,
    )(cols, *pieces, vals, in_vmem(own), in_vmem(other))
    return hidden, feat_grad, weight_grad


def solution(mesh):
    in_specs = (
        P(("groups", "row"), None),
        P(),
        P(("groups", "row"), None),
        P(("groups", "row")),
        P(("groups", "row"), None, None, None),
        P(("groups", "row"), None),
    )
    out_specs = (P(("groups", "row"), None), P(("groups", "row"), None), P("groups", None))
    return jax.shard_map(body, mesh=mesh, in_specs=in_specs, out_specs=out_specs, check_vma=False)
```

```python
import jax
import jax.numpy as jnp
from jax import lax
from jax.experimental import pallas as pl
from jax.experimental.pallas import tpu as pltpu
from jax.sharding import PartitionSpec as P

GROUP = 2
GELU_C = 0.7978845608028654
GELU_A = 0.044715
PARAMS = pltpu.CompilerParams(vmem_limit_bytes=12 * 2**20)
SMEM = pl.BlockSpec(memory_space=pltpu.SMEM)
VMEM = pl.BlockSpec(memory_space=pltpu.VMEM)
HBM = pl.BlockSpec(memory_space=pltpu.HBM)


def in_vmem(x):
    return pltpu.with_memory_space_constraint(x, pltpu.VMEM)


def in_hbm(x):
    return pltpu.with_memory_space_constraint(x, pltpu.HBM)


def in_smem(x):
    return pltpu.with_memory_space_constraint(x, pltpu.SMEM)


def run(copies):
    for c in copies:
        c.start()
    for c in copies:
        c.wait()


def stage_kernel(cols, counts, vals, *refs):
    n = (len(refs) - 3) // 2
    plain, refs = refs[:n], refs[n:]
    cols_out, vals_out = refs[:2]
    plain_out = refs[2 : 2 + n]
    counts_in, sems = refs[2 + n :]
    pairs = [(counts, counts_in), (cols, cols_out), (vals, vals_out), *zip(plain, plain_out)]
    run([pltpu.make_async_copy(i, o, sems.at[k]) for k, (i, o) in enumerate(pairs)])
    panels, slots = vals_out.shape[:2]
    for panel in range(panels):

        def clear(slot, carry):
            vals_out[panel, slot] = jnp.zeros(vals_out.shape[2:], vals_out.dtype)
            return carry

        lax.fori_loop(counts_in[panel], slots, clear, 0)


def stage(cols, counts, vals, *plain):
    n = len(plain)
    return pl.pallas_call(
        stage_kernel,
        name="stage",
        compiler_params=PARAMS,
        out_shape=(
            pltpu.SMEM(cols.shape, cols.dtype),
            *(pltpu.VMEM(a.shape, a.dtype) for a in (vals, *plain)),
        ),
        in_specs=[HBM] * (3 + n),
        out_specs=(SMEM,) + (VMEM,) * (1 + n),
        scratch_shapes=[
            pltpu.SMEM(counts.shape, counts.dtype),
            pltpu.SemaphoreType.DMA((3 + n,)),
        ],
    )(*(in_hbm(a) for a in (cols, counts, vals, *plain)))


def unstage_kernel(x, out, sem):
    run([pltpu.make_async_copy(x, out, sem)])


def unstage(x):
    return pl.pallas_call(
        unstage_kernel,
        name="unstage",
        compiler_params=PARAMS,
        out_shape=jax.ShapeDtypeStruct(x.shape, x.dtype),
        in_specs=[VMEM],
        out_specs=HBM,
        scratch_shapes=[pltpu.SemaphoreType.DMA],
    )(in_vmem(x))


def exchange(x, bit, size):
    return lax.ppermute(x, "row", [(i, i ^ bit) for i in range(size)])


def after(x, *others):
    return lax.optimization_barrier((x, *others))[0]


def pack_kernel(*refs):
    out, start = refs[-1], 0
    for r in refs[:-1]:
        out[pl.ds(start, r.shape[0])] = r[...]
        start += r.shape[0]


def pack(arrays):
    if len(arrays) == 1:
        return arrays[0]
    first = arrays[0]
    total = sum(a.shape[0] for a in arrays)
    return pl.pallas_call(
        pack_kernel,
        name="pack",
        compiler_params=PARAMS,
        out_shape=pltpu.VMEM((total, *first.shape[1:]), first.dtype),
        in_specs=[VMEM] * len(arrays),
        out_specs=VMEM,
    )(*(in_vmem(a) for a in arrays))


CORE_GROUPS = ((0, 2, 4, 8), (6, 10), (12, 14))
SUM_BITS = (2, 8, 4)


def row_sum(keep, send, size, bits):
    total = keep + exchange(send, 1, size)
    for bit in bits:
        total = total + exchange(total, bit, size)
    return total


def gather_rows(x, own, size, staged, halves=None):
    sums = None
    if size != 16:
        if halves is not None:
            bits = [1 << k for k in range(1, (size - 1).bit_length())]
            total = row_sum(*halves, size, bits)
            sums = total, exchange(total, 1, size)
        return [((None,), lax.all_gather(x, "row", axis=0, tiled=True))], sums

    def step(value, k):
        return value if halves is None else after(value, totals[k])

    def advance():
        if halves is not None:
            bit = SUM_BITS[len(totals) - 1]
            totals.append(totals[-1] + exchange(totals[-1], bit, size))

    held = {8: exchange(x, 8, size), 4: exchange(x, 4, size)}
    totals = [] if halves is None else [halves[0] + exchange(halves[1], 1, size)]
    held[12] = exchange(step(after(held[8], staged), 0), 4, size)
    held[2] = exchange(x, 2, size)
    held[6] = exchange(held[2], 4, size)
    advance()
    held[10] = exchange(step(held[8], 1), 2, size)
    advance()
    held[14] = exchange(step(held[12], 2), 2, size)
    advance()
    if halves is not None:
        sums = totals[-1], exchange(totals[-1], 1, size)
    held[0] = own
    pieces = [((mask,), held[mask]) for mask in sorted(held)]
    for group in CORE_GROUPS:
        arrays = [held[mask] for mask in group]
        if group is CORE_GROUPS[-1]:
            arrays[0] = step(arrays[0], 3)
        pieces.append((tuple(mask ^ 1 for mask in group), exchange(pack(arrays), 1, size)))
    return pieces, sums


def collect(me, masks, pieces, nodes):
    if nodes is None:
        return pieces[0]
    for each, piece in zip(masks, pieces):
        blocks = piece.shape[0] // len(each)
        for k, mask in enumerate(each):
            start = (me ^ mask) * blocks
            for i in range(blocks):
                nodes[start + i] = piece[k * blocks + i]
    return nodes


def panel_product(cols, vals, nodes, panel):
    total = None
    for b in range(0, vals.shape[1], GROUP):
        group = range(b, b + GROUP)
        part = jnp.dot(
            jnp.concatenate([vals[panel, i] for i in group], 1),
            jnp.concatenate([nodes[cols[panel, i]] for i in group], 0),
            preferred_element_type=jnp.float32,
        )
        total = part if total is None else total + part
    return total


def split(x):
    high = x.astype(jnp.bfloat16)
    return high, (x - high.astype(jnp.float32)).astype(jnp.bfloat16)


def dot(a, b, dims):
    return lax.dot_general(a, b, (dims, ((), ())), preferred_element_type=jnp.float32)


def forward_kernel(masks, *refs):
    n = len(masks)
    cols = refs[0]
    pieces = refs[1 : 1 + n]
    vals, weight, out_grad = refs[1 + n : 4 + n]
    hidden, edge, keep, send = refs[4 + n : 8 + n]
    wsum = refs[8 + n]
    me = lax.axis_index("row")
    nodes = collect(me, masks, pieces, refs[9 + n] if n > 1 else None)
    panels, _, side, _ = vals.shape
    half = keep.shape[0]
    w = weight[...]
    ww = jnp.concatenate([w, w], 0)
    left, right = [], []
    for panel in range(panels):
        rows = pl.ds(panel * side, side)
        agg = panel_product(cols, vals, nodes, panel)
        agg_h, agg_l = split(agg)
        z = dot(jnp.concatenate([agg_h, agg_l], 1), ww, ((1,), (0,)))
        zz = z * z
        t = jnp.tanh(z * (GELU_C + (GELU_C * GELU_A) * zz))
        half_up = 0.5 + 0.5 * t
        hidden[rows, :] = (z * half_up).astype(jnp.bfloat16)
        slope = half_up + (0.5 * z) * (1.0 - t * t) * (GELU_C + (3.0 * GELU_C * GELU_A) * zz)
        dz = out_grad[rows, :].astype(jnp.float32) * slope
        dz_h, dz_l = split(dz)
        edge[panel] = (dot(dz_h, w, ((1,), (1,))) + dot(dz_l, w, ((1,), (1,)))).astype(jnp.bfloat16)
        left += [agg_h, agg_l, agg_h]
        right += [dz_h, dz_h, dz_l]
    wsum[...] = dot(jnp.concatenate(left, 0), jnp.concatenate(right, 0), ((0,), (0,)))
    core = me % 2
    keep[...] = wsum[pl.ds(pl.multiple_of(core * half, half), half), :]
    send[...] = wsum[pl.ds(pl.multiple_of((1 - core) * half, half), half), :]


def backward_kernel(masks, *refs):
    n = len(masks)
    cols = refs[0]
    pieces = refs[1 : 1 + n]
    vals, own, other = refs[1 + n : 4 + n]
    feat, weight_grad, rows, sems = refs[4 + n : 8 + n]
    me = lax.axis_index("row")
    panels, _, side, _ = vals.shape
    half = own.shape[0]
    copies = []

    def send(source, target):
        copies.append(pltpu.make_async_copy(source, target, sems.at[len(copies)]))
        copies[-1].start()

    core = me % 2
    send(own, weight_grad.at[pl.ds(pl.multiple_of(core * half, half), half)])
    send(other, weight_grad.at[pl.ds(pl.multiple_of((1 - core) * half, half), half)])
    nodes = collect(me, masks, pieces, refs[8 + n] if n > 1 else None)
    for panel in range(panels):
        here = pl.ds(panel * side, side)
        rows[here, :] = panel_product(cols, vals, nodes, panel).astype(jnp.bfloat16)
        send(rows.at[here], feat.at[here])
    for c in copies:
        c.wait()


def body(features, weight, block_cols, block_counts, block_vals, out_grad):
    size = lax.axis_size("row")
    panels, _, side, _ = block_vals.shape
    rows, width = features.shape
    hidden_width = weight.shape[1]
    node_blocks = size * panels
    features_in = features.reshape(panels, side, width)
    cols, vals, out_grad, weight, own_rows = stage(
        block_cols, block_counts, block_vals, out_grad, weight, features_in
    )
    cols, vals = in_smem(cols), in_vmem(vals)

    def gathered(*arrays):
        pieces, sums = gather_rows(*arrays)
        scratch = []
        if len(pieces) > 1:
            scratch = [pltpu.VMEM((node_blocks, side, width), jnp.bfloat16)]
        return sums, tuple(m for m, _ in pieces), [in_vmem(a) for _, a in pieces], scratch

    _, masks, pieces, scratch = gathered(features_in, own_rows, size, own_rows)
    hidden, edge, keep, send = pl.pallas_call(
        lambda *refs: forward_kernel(masks, *refs),
        name="forward",
        compiler_params=PARAMS,
        out_shape=(
            pltpu.VMEM((rows, hidden_width), jnp.bfloat16),
            pltpu.VMEM((panels, side, width), jnp.bfloat16),
            pltpu.VMEM((width // 2, hidden_width), jnp.float32),
            pltpu.VMEM((width // 2, hidden_width), jnp.float32),
        ),
        in_specs=[SMEM] + [VMEM] * (len(pieces) + 3),
        out_specs=(VMEM,) * 4,
        scratch_shapes=[pltpu.VMEM((width, hidden_width), jnp.float32)] + scratch,
    )(cols, *pieces, vals, in_vmem(weight), in_vmem(out_grad))

    hidden = unstage(hidden)
    (own, other), masks, pieces, scratch = gathered(edge, edge, size, hidden, (keep, send))
    feat_grad, weight_grad = pl.pallas_call(
        lambda *refs: backward_kernel(masks, *refs),
        name="backward",
        compiler_params=PARAMS,
        out_shape=(
            jax.ShapeDtypeStruct((rows, width), jnp.bfloat16),
            jax.ShapeDtypeStruct((width, hidden_width), jnp.float32),
        ),
        in_specs=[SMEM] + [VMEM] * (len(pieces) + 3),
        out_specs=(HBM, HBM),
        scratch_shapes=[
            pltpu.VMEM((rows, width), jnp.bfloat16),
            pltpu.SemaphoreType.DMA((panels + 2,)),
        ]
        + scratch,
    )(cols, *pieces, vals, in_vmem(own), in_vmem(other))
    return hidden, feat_grad, weight_grad


def solution(mesh):
    in_specs = (
        P(("groups", "row"), None),
        P(),
        P(("groups", "row"), None),
        P(("groups", "row")),
        P(("groups", "row"), None, None, None),
        P(("groups", "row"), None),
    )
    out_specs = (P(("groups", "row"), None), P(("groups", "row"), None), P("groups", None))
    return jax.shard_map(body, mesh=mesh, in_specs=in_specs, out_specs=out_specs, check_vma=False)
```
